32 devices in a mesh: seq: 16 (over z, x, core), head: 2 (over y).
Axes of the slice: x: 2, y: 2, z: 4, core: 2. Of those that a mesh axis runs over, the one named last changes fastest.
Arguments:
- alignment_rows: bfloat16 [128, 1024, 256], P('seq'), may hold values from -16 to 16
- upstream_derivative_tensor: bfloat16 [128, 1024, 256], P(None, 'seq'), may hold values from -12 to 12
- saved_pair_bias: bfloat16 [8, 1024, 1024], P('head', 'seq'), may hold values from -360 to 360
- pairwise_features: bfloat16 [1024, 1024, 128], P('seq', 'head'), may hold values from -16 to 16
- sequence_layernorm_scaling: float32 [256], replicated, may hold values from 0.5 to 2
- sequence_layernorm_centre: float32 [256], replicated, may hold values from -1 to 1
- asking_projection_matrix: bfloat16 [256, 256], replicated, may hold values from -0.375 to 0.375
- matching_projection_matrix: bfloat16 [256, 256], replicated, may hold values from -0.375 to 0.375
- content_projection_matrix: bfloat16 [256, 256], replicated, may hold values from -0.375 to 0.375
- sigmoid_projection_matrix: bfloat16 [256, 256], replicated, may hold values from -0.375 to 0.375
- gate_offset_bias: float32 [256], replicated, may hold values from -2 to 2
- final_projection_matrix: bfloat16 [256, 256], replicated, may hold values from -0.375 to 0.375
- pairwise_norm_gain: float32 [128], replicated, may hold values from 0.5 to 2
- pairwise_weight: bfloat16 [128, 8], replicated, may hold values from -0.5 to 0.5
Outputs:
- alignment_input_gradient: bfloat16 [128, 1024, 256], P('seq', 'head')
- pairwise_gradient: bfloat16 [1024, 1024, 128], P('seq', 'head')
The draws below stay inside these ranges and needn't reach their ends.
All inputs are finite; a program needn't handle non-finite values.
Results may differ from the reference program's by a relative error of at most 0.012.
The reference program's roundings to bfloat16 on the way count: a program that leaves them out, or rounds other values in their place, can miss the bound.
Values may be sent and summed in bfloat16 or wider, within the bound.
A program may use at most 320 MiB of HBM per device.

```python
import math
import jax
import jax.numpy as jnp
from jax import lax

EMBED_DEPTH = 256
CZ = 128
ATTENTION_TALLY = 8
SUBSPACE_WIDTH = 32
CROP_LENGTH = 1024
SEQUENCE_TALLY = 128


def draw_alignment_rows(key, part):
    base_key = jax.random.fold_in(key, 11)
    random_seed_handle, magnitude_seed_handle = jax.random.split(base_key, 2)
    column_multiplier = jnp.exp(jax.random.uniform(magnitude_seed_handle, (EMBED_DEPTH,), jnp.float32, math.log(0.3), math.log(3.0)))
    tensor_entry = jnp.clip(jax.random.normal(random_seed_handle, (SEQUENCE_TALLY, CROP_LENGTH, EMBED_DEPTH), jnp.float32), -4.0, 4.0)
    return (tensor_entry * column_multiplier).astype(jnp.bfloat16)


def draw_pairwise_features(key, part):
    base_key = jax.random.fold_in(key, 23)
    random_seed_handle, magnitude_seed_handle = jax.random.split(base_key, 2)
    column_multiplier = jnp.exp(jax.random.uniform(magnitude_seed_handle, (CZ,), jnp.float32, math.log(0.3), math.log(3.0)))
    tensor_entry = jnp.clip(jax.random.normal(random_seed_handle, (CROP_LENGTH, CROP_LENGTH, CZ), jnp.float32), -4.0, 4.0)
    return (tensor_entry * column_multiplier).astype(jnp.bfloat16)


def draw_saved_pair_bias(key, part):
    base_key = jax.random.fold_in(key, 37)
    random_seed_handle = jax.random.fold_in(base_key, 0)
    tensor_entry = jnp.clip(0.4 * jax.random.normal(random_seed_handle, (ATTENTION_TALLY, CROP_LENGTH, CROP_LENGTH), jnp.float32), -1.6, 1.6)
    return tensor_entry.astype(jnp.bfloat16)


def strengthened(drawn, stream_key, source, target, parts, factor):
    owner, partner = [(jnp.arange(drawn.shape[axis_at]) // (drawn.shape[axis_at] // parts)).reshape([-1 if axis == axis_at else 1 for axis in range(drawn.ndim)]) for axis_at in (source, target)]
    chosen = jax.random.permutation(stream_key, parts)[partner]
    strong = (owner == chosen) | (owner == (partner + parts // 2) % parts)
    return jnp.where(strong, factor * drawn, drawn)


def levels(own_key, shape, shards, least, largest):
    level = 1.0
    for axis_at, shards_of in shards:
        heights = jax.random.uniform(jax.random.fold_in(jax.random.fold_in(own_key, 6), axis_at), (shards_of,), jnp.float32, least / len(shards), largest / len(shards))
        level = level * jnp.repeat(jnp.exp(heights), shape[axis_at] // shards_of).reshape((-1,) + (1,) * (len(shape) - 1 - axis_at))
    return level


def scatter_about(rng, dims, width, limit, shards=(), kind=jnp.bfloat16):
    drawn = jax.random.normal(rng, dims, jnp.float32) * width
    if len(shards) > 0:
        drawn = levels(rng, dims, shards, -0.22, 0.18) * drawn
    return jnp.clip(drawn, min=-limit, max=limit).astype(kind)


def heavy_noise(rng, dims, width, reach, pieces, heavy, held_as=jnp.bfloat16):
    array = width * jax.random.normal(rng, dims, jnp.float32)
    if pieces:
        array = array * levels(rng, dims, pieces, -0.22, 0.18)
    return jnp.clip(strengthened(array, jax.random.fold_in(rng, 3), *heavy), -reach, reach).astype(held_as)


def setup_inputs(seed: int = 0) -> dict:
    key_of = jax.random.split(jax.random.key(seed), 15)
    alignment_rows = draw_alignment_rows(jax.random.fold_in(key_of[14], 71), 0)
    upstream_derivative_tensor = heavy_noise(key_of[1], (SEQUENCE_TALLY, CROP_LENGTH, EMBED_DEPTH), 2.0, 12.0, ((1, 16),), (0, 1, 16, 2.0))
    saved_pair_bias = draw_saved_pair_bias(jax.random.fold_in(key_of[14], 71), 0)
    pairwise_features = draw_pairwise_features(jax.random.fold_in(key_of[14], 71), 0)
    sequence_layernorm_scaling = jnp.clip(jnp.exp(jax.random.uniform(key_of[4], (EMBED_DEPTH,), jnp.float32, math.log(0.5), math.log(2.0))), 0.5, 2.0)
    sequence_layernorm_centre = jnp.clip(jax.random.uniform(key_of[5], (EMBED_DEPTH,), jnp.float32, -1.0, 1.0), -1.0, 1.0)
    asking_projection_matrix = scatter_about(key_of[6], (EMBED_DEPTH, ATTENTION_TALLY * SUBSPACE_WIDTH), EMBED_DEPTH ** -0.5, 0.375)
    matching_projection_matrix = scatter_about(key_of[7], (EMBED_DEPTH, ATTENTION_TALLY * SUBSPACE_WIDTH), EMBED_DEPTH ** -0.5, 0.375)
    content_projection_matrix = scatter_about(key_of[8], (EMBED_DEPTH, ATTENTION_TALLY * SUBSPACE_WIDTH), EMBED_DEPTH ** -0.5, 0.375)
    sigmoid_projection_matrix = scatter_about(key_of[9], (EMBED_DEPTH, ATTENTION_TALLY * SUBSPACE_WIDTH), EMBED_DEPTH ** -0.5, 0.375)
    gate_offset_bias = jnp.clip(jax.random.uniform(key_of[10], (ATTENTION_TALLY * SUBSPACE_WIDTH,), jnp.float32, -2.0, 2.0), -2.0, 2.0)
    final_projection_matrix = scatter_about(key_of[11], (ATTENTION_TALLY * SUBSPACE_WIDTH, EMBED_DEPTH), (ATTENTION_TALLY * SUBSPACE_WIDTH) ** -0.5, 0.375)
    pairwise_norm_gain = jnp.clip(jnp.exp(jax.random.uniform(key_of[12], (CZ,), jnp.float32, math.log(0.5), math.log(2.0))), 0.5, 2.0)
    pairwise_weight = scatter_about(key_of[13], (CZ, ATTENTION_TALLY), CZ ** -0.5, 0.5)
    return dict(alignment_rows=alignment_rows, upstream_derivative_tensor=upstream_derivative_tensor, saved_pair_bias=saved_pair_bias, pairwise_features=pairwise_features, sequence_layernorm_scaling=sequence_layernorm_scaling, sequence_layernorm_centre=sequence_layernorm_centre, asking_projection_matrix=asking_projection_matrix, matching_projection_matrix=matching_projection_matrix, content_projection_matrix=content_projection_matrix, sigmoid_projection_matrix=sigmoid_projection_matrix, gate_offset_bias=gate_offset_bias, final_projection_matrix=final_projection_matrix, pairwise_norm_gain=pairwise_norm_gain, pairwise_weight=pairwise_weight)


epsilon = 1e-05

def layer_statistics(values):
    average = lax.optimization_barrier(jnp.mean(values, axis=-1, keepdims=True))
    centred = values - average
    inverse_deviation = lax.rsqrt(lax.optimization_barrier(jnp.mean(centred * centred, axis=-1, keepdims=True)) + epsilon)
    return (centred * inverse_deviation, inverse_deviation)

def layer_reverse_step(upstream, standardized_values, inverse_deviation):
    first_mean = lax.optimization_barrier(jnp.mean(upstream, axis=-1, keepdims=True))
    second_mean = lax.optimization_barrier(jnp.mean(upstream * standardized_values, axis=-1, keepdims=True))
    return inverse_deviation * (upstream - first_mean - standardized_values * second_mean)

def rounded(values):
    return lax.optimization_barrier(values.astype(jnp.bfloat16)).astype(jnp.float32)

def reference(alignment_rows, upstream_derivative_tensor, saved_pair_bias, pairwise_features, sequence_layernorm_scaling, sequence_layernorm_centre, asking_projection_matrix, matching_projection_matrix, content_projection_matrix, sigmoid_projection_matrix, gate_offset_bias, final_projection_matrix, pairwise_norm_gain, pairwise_weight):
    score_scale = SUBSPACE_WIDTH ** (-0.5)
    piled_arrays = jnp.stack([coefficient_matrix.reshape(EMBED_DEPTH, ATTENTION_TALLY, SUBSPACE_WIDTH) for coefficient_matrix in (asking_projection_matrix, matching_projection_matrix, content_projection_matrix, sigmoid_projection_matrix)], axis=2)
    piled_arrays = piled_arrays.reshape(EMBED_DEPTH, ATTENTION_TALLY, 4 * SUBSPACE_WIDTH).astype(jnp.float32)
    bias_float = saved_pair_bias.astype(jnp.float32)

    def row_reverse_step(pair_bias_gradient, layer_inputs):
        alignment_row, row_gradient = layer_inputs
        standardized_values, inverse_deviation = layer_statistics(alignment_row.astype(jnp.float32))
        normalized_rows = (standardized_values * sequence_layernorm_scaling + sequence_layernorm_centre).astype(jnp.bfloat16)
        query = rounded(score_scale * jnp.dot(normalized_rows, asking_projection_matrix, preferred_element_type=jnp.float32)).reshape(CROP_LENGTH, ATTENTION_TALLY, SUBSPACE_WIDTH)
        keys = rounded(jnp.dot(normalized_rows, matching_projection_matrix, preferred_element_type=jnp.float32)).reshape(CROP_LENGTH, ATTENTION_TALLY, SUBSPACE_WIDTH)
        vals = rounded(jnp.dot(normalized_rows, content_projection_matrix, preferred_element_type=jnp.float32)).reshape(CROP_LENGTH, ATTENTION_TALLY, SUBSPACE_WIDTH)
        gate = jax.nn.sigmoid(jnp.dot(normalized_rows, sigmoid_projection_matrix, preferred_element_type=jnp.float32) + gate_offset_bias).reshape(CROP_LENGTH, ATTENTION_TALLY, SUBSPACE_WIDTH)
        gated_grad = rounded(jnp.dot(row_gradient, final_projection_matrix.T, preferred_element_type=jnp.float32)).reshape(CROP_LENGTH, ATTENTION_TALLY, SUBSPACE_WIDTH)
        logits = jnp.einsum('ihd,jhd->hij', query, keys) + bias_float
        probs = jax.nn.softmax(logits, axis=-1)
        probs_low = rounded(probs)
        attended = jnp.einsum('hij,jhd->ihd', probs_low, vals)
        attended_grad = rounded(gated_grad * gate)
        gate_grad = rounded(gated_grad * attended * gate * (1.0 - gate))
        prob_grad = jnp.einsum('ihd,jhd->hij', attended_grad, vals)
        inner_sum = lax.optimization_barrier(jnp.sum(probs * prob_grad, axis=-1, keepdims=True))
        score_grad = probs * (prob_grad - inner_sum)
        score_low = rounded(score_grad)
        query_grad = rounded(score_scale * jnp.einsum('hij,jhd->ihd', score_low, keys))
        key_grad = rounded(jnp.einsum('hij,ihd->jhd', score_low, query))
        value_grad = rounded(jnp.einsum('hij,ihd->jhd', probs_low, attended_grad))
        grads = jnp.concatenate([query_grad, key_grad, value_grad, gate_grad], axis=-1)
        normalized_gradient = jnp.einsum('ihf,chf->ic', grads, piled_arrays)
        row_output = layer_reverse_step(normalized_gradient * sequence_layernorm_scaling, standardized_values, inverse_deviation).astype(jnp.bfloat16)
        return (pair_bias_gradient + score_grad, row_output)
    pair_bias_gradient, alignment_input_gradient = lax.scan(row_reverse_step, jnp.zeros((ATTENTION_TALLY, CROP_LENGTH, CROP_LENGTH), jnp.float32), (alignment_rows, upstream_derivative_tensor))
    pair_weight = pairwise_weight.astype(jnp.float32)

    def pair_rows(layer_inputs):
        pair_row, bias_row = layer_inputs
        pair_hat, pair_inv = layer_statistics(pair_row.astype(jnp.float32))
        bias_low = rounded(bias_row)
        pair_normed_grad = jnp.einsum('hj,ch->jc', bias_low, pair_weight, precision=lax.Precision.HIGHEST)
        return layer_reverse_step(pair_normed_grad * pairwise_norm_gain, pair_hat, pair_inv).astype(jnp.bfloat16)
    pairwise_gradient = lax.map(pair_rows, (pairwise_features, jnp.transpose(pair_bias_gradient, (1, 0, 2))))
    return (alignment_input_gradient, pairwise_gradient)
```

```python
import jax
import jax.numpy as jnp
from jax import lax
from jax.experimental import pallas as pl
from jax.experimental.pallas import tpu as pltpu
from jax.sharding import PartitionSpec as P

SUBSPACE_WIDTH = 32


epsilon = 1e-05


def layer_statistics(values):
    average = jnp.mean(values, axis=-1, keepdims=True)
    centred = values - average
    inverse_deviation = lax.rsqrt(jnp.mean(centred * centred, axis=-1, keepdims=True) + epsilon)
    return (centred * inverse_deviation, inverse_deviation)


def layer_reverse_step(upstream, standardized_values, inverse_deviation):
    first_mean = jnp.mean(upstream, axis=-1, keepdims=True)
    second_mean = jnp.mean(upstream * standardized_values, axis=-1, keepdims=True)
    return inverse_deviation * (upstream - first_mean - standardized_values * second_mean)


def dot(left, right, left_dim, right_dim):
    return lax.dot_general(
        left, right, (((left_dim,), (right_dim,)), ((), ())), preferred_element_type=jnp.float32
    )


def attention_kernel(tile, q_ref, k_ref, v_ref, gate_ref, gd_ref, bias_ref, grads_ref, sum_ref, acc_ref):
    score_scale = SUBSPACE_WIDTH ** (-0.5)
    residues = acc_ref.shape[0]

    @pl.when(pl.program_id(0) == 0)
    def _():
        acc_ref[...] = jnp.zeros_like(acc_ref)

    keys_t = k_ref[...]
    vals_t = v_ref[...]
    key_grad = jnp.zeros((SUBSPACE_WIDTH, residues), jnp.float32)
    value_grad = jnp.zeros((SUBSPACE_WIDTH, residues), jnp.float32)
    for start in range(0, residues, tile):
        rows = slice(start, start + tile)
        query_t = q_ref[:, rows]
        query = query_t.astype(jnp.float32).T.astype(jnp.bfloat16)
        logits = dot(query, keys_t, 1, 0) + bias_ref[rows, :].astype(jnp.float32)
        top = jnp.max(logits, axis=-1, keepdims=True)
        weights = jnp.exp(logits - top)
        share = 1.0 / jnp.sum(weights, axis=-1, keepdims=True)
        weights_low = weights.astype(jnp.bfloat16)
        attended = dot(weights_low, vals_t, 1, 1) * share
        gate_t = gate_ref[:, rows]
        grad_t = gd_ref[:, rows].astype(jnp.float32)
        out_grad = (grad_t * gate_t).astype(jnp.bfloat16).astype(jnp.float32).T
        scaled = out_grad * share
        inner = jnp.sum(scaled * attended, axis=-1, keepdims=True)
        prob_grad = dot(scaled.astype(jnp.bfloat16), vals_t, 1, 0)
        score_grad = weights * (prob_grad - inner)
        acc_ref[rows, :] += score_grad
        score_low = score_grad.astype(jnp.bfloat16)
        query_grad = score_scale * dot(score_low, keys_t, 1, 1)
        key_grad += dot(query_t, score_low, 1, 0)
        value_grad += dot(scaled.T.astype(jnp.bfloat16), weights_low, 1, 0)
        gate_grad = grad_t * attended.T * gate_t * (1.0 - gate_t)
        grads_ref[0, :, rows] = query_grad.T.astype(jnp.bfloat16)
        grads_ref[3, :, rows] = gate_grad.astype(jnp.bfloat16)
    grads_ref[1] = key_grad.astype(jnp.bfloat16)
    grads_ref[2] = value_grad.astype(jnp.bfloat16)

    @pl.when(pl.program_id(0) == pl.num_programs(0) - 1)
    def _():
        sum_ref[...] = acc_ref[...].astype(jnp.bfloat16)


def attention_reverse(head, projected, gate, gated_grad, bias_head):
    rows, _, _, width, residues = projected.shape
    tile = 256

    def part(which):
        return pl.BlockSpec(
            (None, None, None, width, residues), lambda s: (s, which, head, 0, 0)
        )

    plain = pl.BlockSpec((None, None, width, residues), lambda s: (s, head, 0, 0))
    square = rows * residues * residues
    return pl.pallas_call(
        lambda *refs: attention_kernel(tile, *refs),
        grid=(rows,),
        in_specs=[
            part(0),
            part(1),
            part(2),
            plain,
            plain,
            pl.BlockSpec((residues, residues), lambda s: (0, 0)),
        ],
        out_specs=[
            pl.BlockSpec((None, 4, width, residues), lambda s: (s, 0, 0, 0)),
            pl.BlockSpec((residues, residues), lambda s: (0, 0)),
        ],
        out_shape=[
            jax.ShapeDtypeStruct((rows, 4, width, residues), jnp.bfloat16),
            jax.ShapeDtypeStruct((residues, residues), jnp.bfloat16),
        ],
        scratch_shapes=[pltpu.VMEM((residues, residues), jnp.float32)],
        cost_estimate=pl.CostEstimate(
            flops=100 * 2 * width * square // 8, bytes_accessed=12 << 20, transcendentals=square
        ),
        compiler_params=pltpu.CompilerParams(vmem_limit_bytes=40 << 20),
        name="attention_reverse_%d" % head,
    )(projected, projected, projected, gate, gated_grad, bias_head)


def per_device(
    alignment_rows,
    upstream_derivative_tensor,
    saved_pair_bias,
    pairwise_features,
    sequence_layernorm_scaling,
    sequence_layernorm_centre,
    asking_projection_matrix,
    matching_projection_matrix,
    content_projection_matrix,
    sigmoid_projection_matrix,
    gate_offset_bias,
    final_projection_matrix,
    pairwise_norm_gain,
    pairwise_weight,
):
    local_heads = saved_pair_bias.shape[0]
    all_heads = pairwise_weight.shape[1]
    resident_rows, residue_total, channel_count = alignment_rows.shape
    head_width = local_heads * SUBSPACE_WIDTH
    first_head = lax.axis_index("head") * local_heads
    first_col = first_head * SUBSPACE_WIDTH
    score_scale = SUBSPACE_WIDTH ** (-0.5)
    biases = [
        lax.all_gather(saved_pair_bias[head], "seq", axis=0, tiled=True)
        for head in range(local_heads)
    ]
    row_grads = lax.all_to_all(
        upstream_derivative_tensor, "seq", split_axis=0, concat_axis=1, tiled=True
    )
    standardized_values, inverse_deviation = layer_statistics(alignment_rows.astype(jnp.float32))
    normalized_rows = (
        standardized_values * sequence_layernorm_scaling + sequence_layernorm_centre
    ).astype(jnp.bfloat16)

    def local(coefficient_matrix):
        return lax.dynamic_slice_in_dim(coefficient_matrix, first_col, head_width, 1)

    stacked = jnp.concatenate(
        [
            local(asking_projection_matrix),
            local(matching_projection_matrix),
            local(content_projection_matrix),
            local(sigmoid_projection_matrix),
        ],
        axis=1,
    )
    raw = jnp.einsum("cf,src->sfr", stacked, normalized_rows, preferred_element_type=jnp.float32)
    factor = jnp.where(jnp.arange(3 * head_width) < head_width, score_scale, 1.0)
    projected = (
        (raw[:, : 3 * head_width] * factor[:, None])
        .astype(jnp.bfloat16)
        .reshape(resident_rows, 3, local_heads, SUBSPACE_WIDTH, residue_total)
    )
    gate_shift = lax.dynamic_slice_in_dim(gate_offset_bias, first_col, head_width, 0)
    channel_shape = (resident_rows, local_heads, SUBSPACE_WIDTH, residue_total)
    gate = jax.nn.sigmoid(raw[:, 3 * head_width :] + gate_shift[:, None]).reshape(channel_shape)
    out_rows = lax.dynamic_slice_in_dim(final_projection_matrix, first_col, head_width, 0)
    gated_grad = (
        jnp.einsum("wc,src->swr", out_rows, row_grads, preferred_element_type=jnp.float32)
        .astype(jnp.bfloat16)
        .reshape(channel_shape)
    )
    head_grads = []
    summed_heads = []
    for head in range(local_heads):
        grads, bias_grad = attention_reverse(head, projected, gate, gated_grad, biases[head])
        head_grads.append(grads)
        summed_heads.append(lax.psum_scatter(bias_grad, "seq", scatter_dimension=0, tiled=True))
    summed_rows = jnp.stack(summed_heads)
    head_grad_rows = jnp.stack(head_grads, axis=1).reshape(
        resident_rows, local_heads, 4 * SUBSPACE_WIDTH, residue_total
    )
    piled_arrays = jnp.stack(
        [
            coefficient_matrix.reshape(channel_count, all_heads, SUBSPACE_WIDTH)
            for coefficient_matrix in (
                asking_projection_matrix,
                matching_projection_matrix,
                content_projection_matrix,
                sigmoid_projection_matrix,
            )
        ],
        axis=2,
    )
    piled_arrays = piled_arrays.reshape(channel_count, all_heads, 4 * SUBSPACE_WIDTH)
    local_weight = lax.dynamic_slice_in_dim(piled_arrays, first_head, local_heads, 1)
    partial_term = jnp.einsum(
        "shfr,chf->src", head_grad_rows, local_weight, preferred_element_type=jnp.float32
    )
    normalized_gradient = lax.psum_scatter(
        partial_term.astype(jnp.bfloat16), "head", scatter_dimension=1, tiled=True
    ).astype(jnp.float32)
    block_len = residue_total // lax.axis_size("head")
    block_start = lax.axis_index("head") * block_len
    normalized_block = lax.dynamic_slice_in_dim(standardized_values, block_start, block_len, 1)
    inverse_spread_block = lax.dynamic_slice_in_dim(inverse_deviation, block_start, block_len, 1)
    alignment_input_gradient = layer_reverse_step(
        normalized_gradient * sequence_layernorm_scaling, normalized_block, inverse_spread_block
    ).astype(jnp.bfloat16)
    bias_tile = lax.all_to_all(
        summed_rows.astype(jnp.bfloat16), "head", split_axis=2, concat_axis=0, tiled=True
    ).astype(summed_rows.dtype)
    bias_low = bias_tile.astype(jnp.bfloat16)
    pair_hat, pair_inv = layer_statistics(pairwise_features.astype(jnp.float32))
    pair_normed_grad = jnp.einsum(
        "hij,ch->ijc", bias_low, pairwise_weight, preferred_element_type=jnp.float32
    )
    pairwise_gradient = layer_reverse_step(
        pair_normed_grad * pairwise_norm_gain, pair_hat, pair_inv
    ).astype(jnp.bfloat16)
    return (alignment_input_gradient, pairwise_gradient)


def solution(mesh):
    placed = (
        P("seq", None, None),
        P(None, "seq", None),
        P("head", "seq", None),
        P("seq", "head", None),
        P(),
        P(),
        P(),
        P(),
        P(),
        P(),
        P(),
        P(),
        P(),
        P(),
    )
    return jax.shard_map(
        per_device,
        mesh=mesh,
        in_specs=placed,
        out_specs=(P("seq", "head", None), P("seq", "head", None)),
        check_vma=False,
    )
```

```python
import jax
import jax.numpy as jnp
from jax import lax
from jax.experimental import pallas as pl
from jax.experimental.pallas import tpu as pltpu
from jax.sharding import PartitionSpec as P

SUBSPACE_WIDTH = 32


epsilon = 1e-05


def layer_statistics(values):
    average = jnp.mean(values, axis=-1, keepdims=True)
    centred = values - average
    inverse_deviation = lax.rsqrt(jnp.mean(centred * centred, axis=-1, keepdims=True) + epsilon)
    return (centred * inverse_deviation, inverse_deviation)


def layer_reverse_step(upstream, standardized_values, inverse_deviation):
    first_mean = jnp.mean(upstream, axis=-1, keepdims=True)
    second_mean = jnp.mean(upstream * standardized_values, axis=-1, keepdims=True)
    return inverse_deviation * (upstream - first_mean - standardized_values * second_mean)


def dot(left, right, left_dim, right_dim):
    return lax.dot_general(
        left, right, (((left_dim,), (right_dim,)), ((), ())), preferred_element_type=jnp.float32
    )


def attention_kernel(tile, q_ref, k_ref, v_ref, gate_ref, gd_ref, bias_ref, grads_ref, sum_ref, acc_ref):
    score_scale = SUBSPACE_WIDTH ** (-0.5)
    residues = acc_ref.shape[0]

    @pl.when(pl.program_id(0) == 0)
    def _():
        acc_ref[...] = jnp.zeros_like(acc_ref)

    keys_t = k_ref[...]
    vals_t = v_ref[...]
    key_grad = jnp.zeros((SUBSPACE_WIDTH, residues), jnp.float32)
    value_grad = jnp.zeros((SUBSPACE_WIDTH, residues), jnp.float32)
    for start in range(0, residues, tile):
        rows = slice(start, start + tile)
        query_t = q_ref[:, rows]
        query = query_t.astype(jnp.float32).T.astype(jnp.bfloat16)
        logits = dot(query, keys_t, 1, 0) + bias_ref[rows, :].astype(jnp.float32)
        top = jnp.max(logits, axis=-1, keepdims=True)
        weights = jnp.exp(logits - top)
        share = 1.0 / jnp.sum(weights, axis=-1, keepdims=True)
        weights_low = weights.astype(jnp.bfloat16)
        attended = dot(weights_low, vals_t, 1, 1) * share
        gate_t = gate_ref[:, rows]
        grad_t = gd_ref[:, rows].astype(jnp.float32)
        out_grad = (grad_t * gate_t).astype(jnp.bfloat16).astype(jnp.float32).T
        scaled = out_grad * share
        inner = jnp.sum(scaled * attended, axis=-1, keepdims=True)
        prob_grad = dot(scaled.astype(jnp.bfloat16), vals_t, 1, 0)
        score_grad = weights * (prob_grad - inner)
        acc_ref[rows, :] += score_grad
        score_low = score_grad.astype(jnp.bfloat16)
        query_grad = score_scale * dot(score_low, keys_t, 1, 1)
        key_grad += dot(query_t, score_low, 1, 0)
        value_grad += dot(scaled.T.astype(jnp.bfloat16), weights_low, 1, 0)
        gate_grad = grad_t * attended.T * gate_t * (1.0 - gate_t)
        grads_ref[0, :, rows] = query_grad.T.astype(jnp.bfloat16)
        grads_ref[3, :, rows] = gate_grad.astype(jnp.bfloat16)
    grads_ref[1] = key_grad.astype(jnp.bfloat16)
    grads_ref[2] = value_grad.astype(jnp.bfloat16)

    @pl.when(pl.program_id(0) == pl.num_programs(0) - 1)
    def _():
        sum_ref[...] = acc_ref[...].astype(jnp.bfloat16)


def attention_reverse(head, projected, gate, gated_grad, bias_head):
    rows, _, _, width, residues = projected.shape
    tile = 256

    def part(which):
        return pl.BlockSpec(
            (None, None, None, width, residues), lambda s: (s, which, head, 0, 0)
        )

    plain = pl.BlockSpec((None, None, width, residues), lambda s: (s, head, 0, 0))
    square = rows * residues * residues
    return pl.pallas_call(
        lambda *refs: attention_kernel(tile, *refs),
        grid=(rows,),
        in_specs=[
            part(0),
            part(1),
            part(2),
            plain,
            plain,
            pl.BlockSpec((residues, residues), lambda s: (0, 0)),
        ],
        out_specs=[
            pl.BlockSpec((None, 4, width, residues), lambda s: (s, 0, 0, 0)),
            pl.BlockSpec((residues, residues), lambda s: (0, 0)),
        ],
        out_shape=[
            jax.ShapeDtypeStruct((rows, 4, width, residues), jnp.bfloat16),
            jax.ShapeDtypeStruct((residues, residues), jnp.bfloat16),
        ],
        scratch_shapes=[pltpu.VMEM((residues, residues), jnp.float32)],
        cost_estimate=pl.CostEstimate(
            flops=100 * 2 * width * square // 8, bytes_accessed=12 << 20, transcendentals=square
        ),
        compiler_params=pltpu.CompilerParams(vmem_limit_bytes=40 << 20),
        name="attention_reverse_%d" % head,
    )(projected, projected, projected, gate, gated_grad, bias_head)


def pair_layout():
    size = lax.axis_size("seq")
    swap = [(index, index ^ 1) for index in range(size)]
    groups = [list(range(minor, size, 2)) for minor in range(2)]
    return swap, groups, lax.axis_index("seq") % 2


def gather_bias(block):
    swap, groups, minor = pair_layout()
    own = lax.all_gather(block, "seq", axis_index_groups=groups, axis=0, tiled=False)
    other = lax.ppermute(own, "seq", swap)
    first = jnp.where(minor == 0, own, other)
    second = jnp.where(minor == 0, other, own)
    return jnp.stack([first, second], axis=1).reshape(-1, block.shape[1])


def scatter_sum(bias_grad):
    swap, groups, minor = pair_layout()
    size = lax.axis_size("seq")
    residues = bias_grad.shape[1]
    blocks = bias_grad.reshape(size // 2, 2, residues // size, residues)
    mine = lax.dynamic_index_in_dim(blocks, minor, 1, keepdims=False)
    theirs = lax.dynamic_index_in_dim(blocks, 1 - minor, 1, keepdims=False)
    received = lax.ppermute(theirs, "seq", swap)
    half = (mine.astype(jnp.float32) + received.astype(jnp.float32)).astype(jnp.bfloat16)
    return lax.psum_scatter(
        half.reshape(-1, residues),
        "seq",
        axis_index_groups=groups,
        scatter_dimension=0,
        tiled=True,
    )


def project_back_kernel(weight_ref, *refs):
    stacked = jnp.concatenate([ref[...] for ref in refs[:-1]], axis=0)
    refs[-1][...] = dot(weight_ref[...], stacked, 1, 0).T.astype(jnp.bfloat16)


def project_back(weight, head_grads):
    rows, width, residues = head_grads[0].shape
    channels = weight.shape[0]
    return pl.pallas_call(
        project_back_kernel,
        grid=(rows,),
        in_specs=[pl.BlockSpec(weight.shape, lambda s: (0, 0))]
        + [pl.BlockSpec((None, width, residues), lambda s: (s, 0, 0))] * len(head_grads),
        out_specs=pl.BlockSpec((None, residues, channels), lambda s: (s, 0, 0)),
        out_shape=jax.ShapeDtypeStruct((rows, residues, channels), jnp.bfloat16),
        compiler_params=pltpu.CompilerParams(vmem_limit_bytes=24 << 20),
        name="project_back",
    )(weight, *head_grads)


def per_device(
    alignment_rows,
    upstream_derivative_tensor,
    saved_pair_bias,
    pairwise_features,
    sequence_layernorm_scaling,
    sequence_layernorm_centre,
    asking_projection_matrix,
    matching_projection_matrix,
    content_projection_matrix,
    sigmoid_projection_matrix,
    gate_offset_bias,
    final_projection_matrix,
    pairwise_norm_gain,
    pairwise_weight,
):
    local_heads = saved_pair_bias.shape[0]
    all_heads = pairwise_weight.shape[1]
    resident_rows, residue_total, channel_count = alignment_rows.shape
    head_width = local_heads * SUBSPACE_WIDTH
    first_head = lax.axis_index("head") * local_heads
    first_col = first_head * SUBSPACE_WIDTH
    score_scale = SUBSPACE_WIDTH ** (-0.5)
    biases = [
        gather_bias(saved_pair_bias[head])
        for head in range(local_heads)
    ]
    row_grads = lax.all_to_all(
        upstream_derivative_tensor, "seq", split_axis=0, concat_axis=1, tiled=True
    )
    standardized_values, inverse_deviation = layer_statistics(alignment_rows.astype(jnp.float32))
    normalized_rows = (
        standardized_values * sequence_layernorm_scaling + sequence_layernorm_centre
    ).astype(jnp.bfloat16)

    def local(coefficient_matrix):
        return lax.dynamic_slice_in_dim(coefficient_matrix, first_col, head_width, 1)

    stacked = jnp.concatenate(
        [
            local(asking_projection_matrix),
            local(matching_projection_matrix),
            local(content_projection_matrix),
            local(sigmoid_projection_matrix),
        ],
        axis=1,
    )
    raw = jnp.einsum("cf,src->sfr", stacked, normalized_rows, preferred_element_type=jnp.float32)
    factor = jnp.where(jnp.arange(3 * head_width) < head_width, score_scale, 1.0)
    projected = (
        (raw[:, : 3 * head_width] * factor[:, None])
        .astype(jnp.bfloat16)
        .reshape(resident_rows, 3, local_heads, SUBSPACE_WIDTH, residue_total)
    )
    gate_shift = lax.dynamic_slice_in_dim(gate_offset_bias, first_col, head_width, 0)
    channel_shape = (resident_rows, local_heads, SUBSPACE_WIDTH, residue_total)
    gate = jax.nn.sigmoid(raw[:, 3 * head_width :] + gate_shift[:, None]).reshape(channel_shape)
    out_rows = lax.dynamic_slice_in_dim(final_projection_matrix, first_col, head_width, 0)
    gated_grad = (
        jnp.einsum("wc,src->swr", out_rows, row_grads, preferred_element_type=jnp.float32)
        .astype(jnp.bfloat16)
        .reshape(channel_shape)
    )
    head_grads = []
    summed_heads = []
    for head in range(local_heads):
        grads, bias_grad = attention_reverse(head, projected, gate, gated_grad, biases[head])
        head_grads.append(grads)
        summed_heads.append(scatter_sum(bias_grad))
    summed_rows = jnp.stack(summed_heads)
    piled_arrays = jnp.stack(
        [
            coefficient_matrix.reshape(channel_count, all_heads, SUBSPACE_WIDTH)
            for coefficient_matrix in (
                asking_projection_matrix,
                matching_projection_matrix,
                content_projection_matrix,
                sigmoid_projection_matrix,
            )
        ],
        axis=2,
    )
    piled_arrays = piled_arrays.reshape(channel_count, all_heads, 4 * SUBSPACE_WIDTH)
    local_weight = lax.dynamic_slice_in_dim(piled_arrays, first_head, local_heads, 1)
    partial_term = project_back(
        local_weight.reshape(channel_count, local_heads * 4 * SUBSPACE_WIDTH),
        [
            grads.reshape(resident_rows, 4 * SUBSPACE_WIDTH, residue_total)
            for grads in head_grads
        ],
    )
    normalized_gradient = lax.psum_scatter(
        partial_term.astype(jnp.bfloat16), "head", scatter_dimension=1, tiled=True
    ).astype(jnp.float32)
    block_len = residue_total // lax.axis_size("head")
    block_start = lax.axis_index("head") * block_len
    normalized_block = lax.dynamic_slice_in_dim(standardized_values, block_start, block_len, 1)
    inverse_spread_block = lax.dynamic_slice_in_dim(inverse_deviation, block_start, block_len, 1)
    alignment_input_gradient = layer_reverse_step(
        normalized_gradient * sequence_layernorm_scaling, normalized_block, inverse_spread_block
    ).astype(jnp.bfloat16)
    bias_tile = lax.all_to_all(
        summed_rows.astype(jnp.bfloat16), "head", split_axis=2, concat_axis=0, tiled=True
    ).astype(summed_rows.dtype)
    bias_low = bias_tile.astype(jnp.bfloat16)
    pair_hat, pair_inv = layer_statistics(pairwise_features.astype(jnp.float32))
    pair_normed_grad = jnp.einsum(
        "hij,ch->ijc", bias_low, pairwise_weight, preferred_element_type=jnp.float32
    )
    pairwise_gradient = layer_reverse_step(
        pair_normed_grad * pairwise_norm_gain, pair_hat, pair_inv
    ).astype(jnp.bfloat16)
    return (alignment_input_gradient, pairwise_gradient)


def solution(mesh):
    placed = (
        P("seq", None, None),
        P(None, "seq", None),
        P("head", "seq", None),
        P("seq", "head", None),
        P(),
        P(),
        P(),
        P(),
        P(),
        P(),
        P(),
        P(),
        P(),
        P(),
    )
    return jax.shard_map(
        per_device,
        mesh=mesh,
        in_specs=placed,
        out_specs=(P("seq", "head", None), P("seq", "head", None)),
        check_vma=False,
    )
```
